32 devices in a mesh: seq: 8 (over z, y), head: 4 (over x, core).
Axes of the slice: x: 2, y: 2, z: 4, core: 2. Of those that a mesh axis runs over, the one named last changes fastest.
Arguments:
- queries: bfloat16 [4096, 2048], P('seq', 'head'), may hold values from -6 to 6
- keys: bfloat16 [4096, 2048], P('seq', 'head'), may hold values from -6 to 6
- values: bfloat16 [4096, 2048], P('seq', 'head'), may hold values from -6 to 6
- level_weights: int32 [16, 20], P('head'), may hold values from 1 to 8
- out_grad: bfloat16 [4096, 2048], P('seq'), may hold values from -6 to 6
Outputs:
- normed: bfloat16 [4096, 2048], P('seq', 'head')
- proj_grad: float32 [2048, 2048], P('seq', 'head')
The draws below stay inside these ranges and needn't reach their ends.
All inputs are finite; a program needn't handle non-finite values.
Results may differ from the reference program's by a relative error of at most 0.0031.
Values sent between devices are 32-bit elements; how exact they have to be, the bound alone decides.
A program may use at most 64 MiB of HBM per device.

```python
import jax
import jax.numpy as jnp
from jax import lax

D = 2048
HEADS = 16
HEAD_DIM = 128
GROUP = 512
LEVELS = 20
TOKENS = 4096


def place_ends(entries, own_key, least, top_value):
    shape = entries.shape
    spot = [jax.random.randint(jax.random.fold_in(own_key, axis), (), 0, shape[axis]) for axis in range(len(shape))]
    entries = entries.at[tuple(spot)].set(least)
    longest = shape.index(max(shape))
    spot[longest] = (spot[longest] + 1) % shape[longest]
    return entries.at[tuple(spot)].set(top_value)


def spiked(drawn, stream_key, source, target, shards_of, factor):
    def block_of(axis_at):
        return (jnp.arange(drawn.shape[axis_at]) // (drawn.shape[axis_at] // shards_of)).reshape((-1,) + (1,) * (drawn.ndim - 1 - axis_at))

    first = jax.random.permutation(stream_key, shards_of)[block_of(target)]
    other_side = (block_of(target) + shards_of // 2) % shards_of
    return jnp.where((block_of(source) == first) | (block_of(source) == other_side), factor * drawn, drawn)


def levels(rng, extent, shards, least, top_value):
    def one(dim, parts):
        heights = jax.random.uniform(jax.random.fold_in(jax.random.fold_in(rng, 6), dim), (parts,), jnp.float32, least / len(shards), top_value / len(shards))
        return jnp.repeat(jnp.exp(heights), extent[dim] // parts).reshape((-1,) + (1,) * (len(extent) - dim - 1))

    gain = one(*shards[0])
    for cut in shards[1:]:
        gain = gain * one(*cut)
    return gain


def noise(rng, extent, spread, most, pieces=(), kind=jnp.bfloat16):
    values = spread * jax.random.normal(rng, extent, jnp.float32)
    if pieces:
        values = values * levels(rng, extent, pieces, -0.22, 0.18)
    return jnp.clip(values, -most, most).astype(kind)


def heavy_noise(stream_key, extent, deviation, most, pieces, heavy, held_as=jnp.bfloat16):
    entries = deviation * jax.random.normal(stream_key, extent, jnp.float32)
    if pieces:
        entries = entries * levels(stream_key, extent, pieces, -0.22, 0.18)
    return jnp.clip(spiked(entries, jax.random.fold_in(stream_key, 3), *heavy), -most, most).astype(held_as)


def setup_inputs(seed: int = 0) -> dict:
    arg_keys = jax.random.split(jax.random.key(seed), 6)
    return {
        "queries": noise(arg_keys[0], (TOKENS, D), 1.0, 6.0, ((0, 8), (1, 4))),
        "keys": noise(arg_keys[1], (TOKENS, D), 1.0, 6.0, ((0, 8), (1, 4))),
        "values": noise(arg_keys[2], (TOKENS, D), 1.0, 6.0, ((0, 8), (1, 4))),
        "level_weights": place_ends(jax.random.randint(arg_keys[3], (HEADS, LEVELS), 1, 9), jax.random.fold_in(arg_keys[3], 1), 1, 8).astype(jnp.int32),
        "out_grad": heavy_noise(arg_keys[4], (TOKENS, D), 1.0, 6.0, ((0, 8),), (0, 1, 8, 2.0)),
    }


def level_table(count):
    index = jnp.arange(count, dtype=jnp.int32)
    mixed = jnp.bitwise_xor(index[:, None], index[None, :])
    level = jnp.zeros((count, count), jnp.int32)
    for bit in range(LEVELS):
        level = level + (mixed >= 2 ** bit).astype(jnp.int32)
    return (level, index)

def one_head(inputs):
    head_q, head_k, head_v, head_w = inputs
    nchunks = TOKENS // GROUP
    scale = HEAD_DIM ** (-0.5)
    qc = head_q.reshape(nchunks, GROUP, HEAD_DIM).astype(jnp.float32)
    kc = head_k.reshape(nchunks, GROUP, HEAD_DIM).astype(jnp.float32)
    vc = head_v.reshape(nchunks, GROUP, HEAD_DIM)
    vf = vc.astype(jnp.float32)
    weights = head_w.astype(jnp.float32)
    state = jnp.einsum('cnd,cne->cde', kc, vf, precision=lax.Precision.HIGHEST)
    level, index = level_table(nchunks)
    table = jnp.where(index[None, :] < index[:, None], jnp.take(weights, level), 0.0)
    mix = jnp.einsum('cj,jde->cde', table, state, precision=lax.Precision.HIGHEST)
    far = scale * jnp.einsum('cnd,cde->cne', qc, mix, precision=lax.Precision.HIGHEST)
    scores = jnp.einsum('cnd,cmd->cnm', qc, kc, precision=lax.Precision.HIGHEST) * (scale * weights[0])
    rows = jnp.arange(GROUP, dtype=jnp.int32)
    causal = rows[None, :] <= rows[:, None]
    probs = jnp.where(causal[None], scores, 0.0).astype(jnp.bfloat16)
    near = jnp.einsum('cnm,cme->cne', probs.astype(jnp.float32), vf, precision=lax.Precision.HIGHEST)
    return (near + far).reshape(TOKENS, HEAD_DIM)

def reference(queries, keys, values, level_weights, out_grad):

    def split(array):
        return array.reshape(TOKENS, HEADS, HEAD_DIM).transpose(1, 0, 2)
    raw = lax.map(one_head, (split(queries), split(keys), split(values), level_weights))
    raw = raw.transpose(1, 0, 2).reshape(TOKENS, D)
    mean_sq = lax.optimization_barrier(jnp.sum(raw * raw, axis=1)) / D
    normed = (raw * lax.rsqrt(mean_sq + 1e-06)[:, None]).astype(jnp.bfloat16)
    proj_grad = jnp.dot(out_grad.T, normed, preferred_element_type=jnp.float32)
    return (normed, proj_grad)
```

```python
import functools

import jax
import jax.numpy as jnp
from jax import lax
from jax.experimental import pallas as pl
from jax.experimental.pallas import tpu as pltpu
from jax.sharding import PartitionSpec as P

D = 2048
HEADS = 16
GROUP = 512
PIECES = 2
MESH = pl.DeviceIdType.MESH
NT = (((1,), (1,)), ((), ()))
TN = (((0,), (0,)), ((), ()))


def flip(index, mask):
    bit = 1
    while bit <= mask:
        if mask & bit:
            index = index + bit - 2 * bit * ((index // bit) % 2)
        bit *= 2
    return index


def matmul(a, b, dims=(((1,), (0,)), ((), ()))):
    return lax.dot_general(a, b, dims, preferred_element_type=jnp.float32)


def split(x):
    high = x.astype(jnp.bfloat16)
    return high, (x - high.astype(jnp.float32)).astype(jnp.bfloat16)


def kernel(
    line,
    heads,
    q_in,
    k_in,
    v_in,
    level_ref,
    grad_in,
    normed_ref,
    out_ref,
    q_ref,
    k_ref,
    v_ref,
    grad_ref,
    loads,
    state,
    pair_state,
    block,
    line_state,
    give,
    mix,
    turned,
    quarter,
    theirs,
    theirs_half,
    raw,
    came,
    squares,
    squares_in,
    root,
    root_in,
    part,
    rising,
    falling,
    state_send,
    state_recv,
    grad_send,
    grad_recv,
    square_send,
    square_recv,
    root_send,
    root_recv,
    pair_send,
    pair_recv,
    up_send,
    up_recv,
    down_send,
    down_recv,
):
    me = lax.axis_index("seq")
    head = lax.axis_index("head")
    place = me // 2
    side = me % 2
    other = flip(me, 1)
    above = me + 2
    below = me - 2
    tokens, width = q_ref.shape
    lanes = D // HEADS
    chunks = width // lanes
    half = chunks // 2
    rows = out_ref.shape[0]
    line_bits = line.bit_length() - 1
    head_bits = heads.bit_length() - 1
    share = line // heads
    piece = rows // PIECES
    stages = list(reversed(range(head_bits)))
    held = [[0]]
    for bit in stages:
        held.append(held[-1] + [r ^ (1 << bit) for r in held[-1]])
    scale = lanes ** (-0.5)
    low_end = place == 0
    high_end = place == line - 1

    def span(k):
        return slice(k * lanes, (k + 1) * lanes)

    pairs = ((k_in, k_ref), (v_in, v_ref), (grad_in, grad_ref), (q_in, q_ref))
    copies = [pltpu.make_async_copy(a, b, loads.at[i]) for i, (a, b) in enumerate(pairs)]
    for copy in copies:
        copy.start()

    barrier = pltpu.get_barrier_semaphore()

    def greet(device):
        pl.semaphore_signal(barrier, inc=1, device_id=device, device_id_type=MESH)

    greet({"seq": other})
    for b in range(line_bits):
        greet({"seq": flip(me, 2 << b)})
    for r in range(1, heads):
        greet({"head": flip(head, r)})

    @pl.when(place < line - 1)
    def _():
        greet({"seq": above})

    @pl.when(place > 0)
    def _():
        greet({"seq": below})

    def remote(src, dst, send, recv, device):
        return pltpu.make_async_remote_copy(
            src_ref=src,
            dst_ref=dst,
            send_sem=send,
            recv_sem=recv,
            device_id=device,
            device_id_type=MESH,
        )

    def state_copy():
        return remote(
            state.at[pl.ds((1 - side) * half, half)],
            pair_state,
            state_send.at[0],
            state_recv.at[0],
            {"seq": other},
        )

    def line_copy(b):
        return remote(
            block.at[b],
            line_state.at[b],
            state_send.at[1 + b],
            state_recv.at[1 + b],
            {"seq": flip(me, 2 << b)},
        )

    def give_copy():
        return remote(
            give,
            mix.at[pl.ds(side * half, half)],
            state_send.at[1 + line_bits],
            state_recv.at[1 + line_bits],
            {"seq": other},
        )

    def grad_copy(p):
        return remote(
            quarter.at[:, pl.ds(p * piece, piece)],
            theirs.at[pl.ds(head * share, share), pl.ds(p * piece, piece)],
            grad_send.at[0, p],
            grad_recv.at[0, p],
            {"seq": other},
        )

    def share_copy(r, bit, p):
        owned = theirs.at[pl.ds(flip(head, r) * share, share), pl.ds(p * piece, piece)]
        slot = r ^ (1 << bit)
        return remote(
            owned,
            owned,
            grad_send.at[slot, p],
            grad_recv.at[slot, p],
            {"head": flip(head, 1 << bit)},
        )

    def square_copy(r):
        return remote(
            squares,
            squares_in.at[r - 1],
            square_send.at[r - 1],
            square_recv.at[r - 1],
            {"head": flip(head, r)},
        )

    def root_copy():
        return remote(root, root_in, root_send.at[0], root_recv.at[0], {"seq": other})

    def pair_copy(k):
        return remote(raw.at[k], came.at[k], pair_send.at[k], pair_recv.at[k], {"seq": other})

    def up_copy(k, d):
        return remote(
            part.at[k, d], rising.at[k, d], up_send.at[k, d], up_recv.at[k, d], {"seq": above}
        )

    def down_copy(k, d):
        return remote(
            part.at[k, d], falling.at[k, d], down_send.at[k, d], down_recv.at[k, d], {"seq": below}
        )

    copies[0].wait()
    copies[1].wait()
    for h in range(chunks):
        state[h] = matmul(k_ref[:, span(h)], v_ref[:, span(h)], TN)
    peers = line_bits + heads + jnp.where(place > 0, 1, 0) + jnp.where(place < line - 1, 1, 0)
    pl.semaphore_wait(barrier, peers)
    state_copy().start()

    copies[2].wait()
    tile = max(rows, lanes)
    for j in range(grad_ref.shape[1] // tile):
        flat = grad_ref[:, j * tile : (j + 1) * tile].T
        for i in range(tile // rows):
            owner = j * (tile // rows) + i
            turned[owner % 2, owner // 2] = flat[i * rows : (i + 1) * rows]
    quarter[...] = turned[1 - side, pl.ds(head * share, share)].astype(jnp.float32)
    for p in range(PIECES):
        grad_copy(p).start()

    def forward(i, p):
        for r in held[i]:
            share_copy(r, stages[i], p).start()

    def collect(i, p):
        for r in held[i]:
            share_copy(r, stages[i], p).wait_recv()

    def near(h):
        weight = scale * level_ref[h, 0].astype(jnp.float32)
        scores = matmul(q_ref[:, span(h)], k_ref[:, span(h)], NT) * weight
        row = lax.broadcasted_iota(jnp.int32, scores.shape, 0)
        column = lax.broadcasted_iota(jnp.int32, scores.shape, 1)
        probs = jnp.where(column <= row, scores, 0.0).astype(jnp.bfloat16)
        raw[h] = matmul(probs, v_ref[:, span(h)])

    def level(i, number):
        return level_ref[side * half + i, number].astype(jnp.float32)

    copies[3].wait()
    own = pl.ds(side * half, half)
    state_copy().wait_recv()
    block[0] = state[own] + pair_state[...]
    done = 0
    for b in range(line_bits):
        upper = (place // (1 << b)) % 2
        last = b == line_bits - 1
        if last:

            @pl.when(upper == 0)
            def _():
                line_copy(b).start()
        else:
            line_copy(b).start()
        until = chunks * (b + 1) // line_bits
        for h in range(done, until):
            near(h)
        done = until
        if last:
            grad_copy(0).wait_recv()
            forward(0, 0)

            @pl.when(upper == 1)
            def _():
                line_copy(b).wait_recv()

            @pl.when(upper == 0)
            def _():
                line_state[b] = jnp.zeros(line_state.shape[1:], jnp.float32)
        else:
            line_copy(b).wait_recv()
            block[b + 1] = block[b] + line_state[b]
    for i in range(half):
        far = jnp.zeros((lanes, lanes), jnp.float32)
        for b in range(line_bits):
            upper = ((place // (1 << b)) % 2).astype(jnp.float32)
            far = far + (level(i, 2 + b) * upper) * line_state[b, i]
        first = level(i, 1)
        right = side.astype(jnp.float32)
        mix[side * half + i] = far + (first * right) * pair_state[i]
        give[i] = far + (first * (1.0 - right)) * state[side * half + i]
    give_copy().start()

    for p in range(1, PIECES):
        grad_copy(p).wait_recv()
        forward(0, p)
    give_copy().wait_recv()

    total = jnp.zeros((tokens, lanes), jnp.float32)
    for h in range(chunks):
        high, low = split(mix[h])
        query = q_ref[:, span(h)]
        value = raw[h] + scale * (matmul(query, high) + matmul(query, low))
        raw[h] = value
        if h == 0:
            pair_copy(0).start()
        total = total + value * value
    ones = jnp.ones((8, lanes), jnp.bfloat16)
    high, low = split(total)
    squares[...] = matmul(ones, high, NT) + matmul(ones, low, NT)
    for r in range(1, heads):
        square_copy(r).start()
    collect(0, 0)
    forward(1, 0)
    for r in range(1, heads):
        square_copy(r).wait_recv()
    whole = squares[...]
    for r in range(1, heads):
        whole = whole + squares_in[r - 1]
    root[...] = lax.rsqrt(whole / D + 1e-06)
    root_copy().start()
    for p in range(1, PIECES):
        collect(0, p)
        forward(1, p)
    inverse = root[...].T[:, :1]
    for h in range(chunks):
        normed_ref[:, span(h)] = (raw[h] * inverse).astype(jnp.bfloat16)
    pair_copy(0).wait_send()
    pair_copy(1).start()
    root_copy().wait_recv()
    their_inverse = root_in[...].T[:, :1]
    for i in range(1, head_bits):
        for p in range(PIECES):
            if i > 1:
                forward(i, p)
            collect(i, p)
    theirs_half[...] = theirs[...].reshape(theirs_half.shape).astype(jnp.bfloat16)

    def ends(k):
        @pl.when(low_end)
        def _():
            @pl.loop(0, line - 1)
            def _(i):
                up_copy(k, line - 1 - i).start()

        @pl.when(high_end)
        def _():
            @pl.loop(0, line - 1)
            def _(d):
                down_copy(k, d).start()

    def rise(k):
        @pl.loop(0, line - 1 - place)
        def _(i):
            d = line - 1 - i
            up_copy(k, d).wait_recv()
            part[k, d] = part[k, d] + rising[k, d]
            up_copy(k, d).start()

    def fall(k):
        @pl.loop(0, place)
        def _(d):
            down_copy(k, d).wait_recv()
            part[k, d] = part[k, d] + falling[k, d]
            down_copy(k, d).start()

    def middle(k):
        @pl.when(jnp.logical_and(place > 0, place < line // 2))
        def _():
            rise(k)
            fall(k)

        @pl.when(jnp.logical_and(place >= line // 2, place < line - 1))
        def _():
            fall(k)
            rise(k)

    for k in range(chunks):
        mine = turned[side].reshape(line * rows, tokens)
        product = matmul(mine, normed_ref[:, span(k)])
        if k:
            pair_copy(k).wait_send()
            if k + 1 < chunks:
                pair_copy(k + 1).start()
        pair_copy(k).wait_recv()
        there = (came[k] * their_inverse).astype(jnp.bfloat16)
        product = product + matmul(theirs_half[...], there)
        part[k] = product.reshape(part.shape[1:])
        ends(k)
        if k:
            middle(k - 1)
    middle(chunks - 1)

    for k in range(chunks):
        out_ref[:, span(k)] = part[k, place]

        @pl.when(place > 0)
        def _():
            up_copy(k, place).wait_recv()
            out_ref[:, span(k)] = out_ref[:, span(k)] + rising[k, place]

        @pl.when(place < line - 1)
        def _():
            down_copy(k, place).wait_recv()
            out_ref[:, span(k)] = out_ref[:, span(k)] + falling[k, place]

    state_copy().wait_send()
    for b in range(line_bits - 1):
        line_copy(b).wait_send()

    @pl.when((place // (line // 2)) % 2 == 0)
    def _():
        line_copy(line_bits - 1).wait_send()

    give_copy().wait_send()
    for p in range(PIECES):
        grad_copy(p).wait_send()
        for i in range(head_bits):
            for r in held[i]:
                share_copy(r, stages[i], p).wait_send()
    for r in range(1, heads):
        square_copy(r).wait_send()
    root_copy().wait_send()
    for k in range(chunks):
        @pl.loop(place + 1, line)
        def _(d):
            up_copy(k, d).wait_send()

        @pl.loop(0, place)
        def _(d):
            down_copy(k, d).wait_send()


def body(queries, keys, values, level_weights, out_grad):
    tokens, width = queries.shape
    assert tokens == GROUP
    count = lax.axis_size("seq")
    heads = lax.axis_size("head")
    line = count // 2
    line_bits = line.bit_length() - 1
    lanes = D // HEADS
    chunks = width // lanes
    half = chunks // 2
    rows = out_grad.shape[1] // count
    slots = (chunks, line, rows, lanes)
    states = (half, lanes, lanes)
    vmem = pl.BlockSpec(memory_space=pltpu.VMEM)
    smem = pl.BlockSpec(memory_space=pltpu.SMEM)
    away = pl.BlockSpec(memory_space=pltpu.MemorySpace.HBM)
    f32 = jnp.float32
    dma = pltpu.SemaphoreType.DMA
    return pl.pallas_call(
        functools.partial(kernel, line, heads),
        out_shape=(
            pltpu.VMEM((tokens, width), jnp.bfloat16),
            pltpu.VMEM((rows, width), f32),
        ),
        in_specs=[away, away, away, smem, away],
        out_specs=(vmem, vmem),
        scratch_shapes=[
            pltpu.VMEM(queries.shape, queries.dtype),
            pltpu.VMEM(keys.shape, keys.dtype),
            pltpu.VMEM(values.shape, values.dtype),
            pltpu.VMEM(out_grad.shape, out_grad.dtype),
            pltpu.SemaphoreType.DMA((4,)),
            pltpu.VMEM((chunks, lanes, lanes), f32),
            pltpu.VMEM(states, f32),
            pltpu.VMEM((line_bits, *states), f32),
            pltpu.VMEM((line_bits, *states), f32),
            pltpu.VMEM(states, f32),
            pltpu.VMEM((chunks, lanes, lanes), f32),
            pltpu.VMEM((2, line, rows, tokens), jnp.bfloat16),
            pltpu.VMEM((line // heads, rows, tokens), f32),
            pltpu.VMEM((line, rows, tokens), f32),
            pltpu.VMEM((line * rows, tokens), jnp.bfloat16),
            pltpu.VMEM((chunks, tokens, lanes), f32),
            pltpu.VMEM((chunks, tokens, lanes), f32),
            pltpu.VMEM((8, tokens), f32),
            pltpu.VMEM((heads - 1, 8, tokens), f32),
            pltpu.VMEM((8, tokens), f32),
            pltpu.VMEM((8, tokens), f32),
            pltpu.VMEM(slots, f32),
            pltpu.VMEM(slots, f32),
            pltpu.VMEM(slots, f32),
            dma((2 + line_bits,)),
            dma((2 + line_bits,)),
            dma((heads, PIECES)),
            dma((heads, PIECES)),
            dma((heads - 1,)),
            dma((heads - 1,)),
            dma((1,)),
            dma((1,)),
            dma((chunks,)),
            dma((chunks,)),
            dma((chunks, line)),
            dma((chunks, line)),
            dma((chunks, line)),
            dma((chunks, line)),
        ],
        compiler_params=pltpu.CompilerParams(
            collective_id=0, has_side_effects=True, vmem_limit_bytes=60 << 20
        ),
    )(queries, keys, values, level_weights, out_grad)


def solution(mesh):
    return jax.shard_map(
        body,
        mesh=mesh,
        in_specs=(
            P("seq", "head"),
            P("seq", "head"),
            P("seq", "head"),
            P("head", None),
            P("seq", None),
        ),
        out_specs=(P("seq", "head"), P("seq", "head")),
        check_vma=False,
    )
```

```python
import functools

import jax
import jax.numpy as jnp
from jax import lax
from jax.experimental import pallas as pl
from jax.experimental.pallas import tpu as pltpu
from jax.sharding import PartitionSpec as P

D = 2048
HEADS = 16
GROUP = 512
PIECES = 4
STATE_PIECES = 2
SLOT_PIECES = 2
MESH = pl.DeviceIdType.MESH
NT = (((1,), (1,)), ((), ()))
TN = (((0,), (0,)), ((), ()))


def flip(index, mask):
    bit = 1
    while bit <= mask:
        if mask & bit:
            index = index + bit - 2 * bit * ((index // bit) % 2)
        bit *= 2
    return index


def matmul(a, b, dims=(((1,), (0,)), ((), ()))):
    return lax.dot_general(a, b, dims, preferred_element_type=jnp.float32)


def split(x):
    high = x.astype(jnp.bfloat16)
    return high, (x - high.astype(jnp.float32)).astype(jnp.bfloat16)


def kernel(
    line,
    heads,
    q_in,
    k_in,
    v_in,
    level_ref,
    grad_in,
    normed_ref,
    out_ref,
    q_ref,
    k_ref,
    v_ref,
    grad_ref,
    loads,
    state,
    pair_state,
    block,
    line_state,
    give,
    mix,
    turned,
    quarter,
    theirs,
    theirs_half,
    raw,
    came,
    there,
    squares,
    squares_in,
    part,
    rising,
    falling,
    state_send,
    state_recv,
    grad_send,
    grad_recv,
    square_send,
    square_recv,
    pair_send,
    pair_recv,
    up_send,
    up_recv,
    down_send,
    down_recv,
):
    me = lax.axis_index("seq")
    head = lax.axis_index("head")
    place = me // 2
    side = me % 2
    other = flip(me, 1)
    above = me + 2
    below = me - 2
    tokens, width = q_ref.shape
    lanes = D // HEADS
    chunks = width // lanes
    half = chunks // 2
    rows = out_ref.shape[0]
    line_bits = line.bit_length() - 1
    head_bits = heads.bit_length() - 1
    group = line // PIECES
    last = PIECES - 1
    token_share = tokens // heads
    part_rows = rows // SLOT_PIECES
    state_rows = lanes // STATE_PIECES
    stages = list(reversed(range(head_bits)))
    held = [[0]]
    for bit in stages:
        held.append(held[-1] + [r ^ (1 << bit) for r in held[-1]])
    state_parts = [(i, s) for i in range(half) for s in range(STATE_PIECES)]
    scale = lanes ** (-0.5)
    low_end = place == 0
    high_end = place == line - 1

    def span(k):
        return slice(k * lanes, (k + 1) * lanes)

    def columns(k):
        return pl.ds(pl.multiple_of(k * lanes, lanes), lanes)

    def bit_of(b):
        return (place // (1 << b)) % 2

    def ends_block(b):
        return place % (1 << b) == (1 << b) - 1

    mine = place // group
    lower = place < line // 2

    def first_slot(p):
        ordered = jnp.where(lower, mine + PIECES - 1 - p, mine + 1 + p)
        return (ordered % PIECES) * group

    def slots(p):
        return pl.ds(first_slot(p), group)

    pairs = ((k_in, k_ref), (v_in, v_ref), (grad_in, grad_ref), (q_in, q_ref))
    copies = [pltpu.make_async_copy(a, b, loads.at[i]) for i, (a, b) in enumerate(pairs)]
    for copy in copies:
        copy.start()

    barrier = pltpu.get_barrier_semaphore()

    def greet(device):
        pl.semaphore_signal(barrier, inc=1, device_id=device, device_id_type=MESH)

    greet({"seq": other})
    for r in range(1, heads):
        greet({"head": flip(head, r)})
        greet({"seq": other, "head": flip(head, r)})

    @pl.when(place < line - 1)
    def _():
        greet({"seq": above})

    @pl.when(place > 0)
    def _():
        greet({"seq": below})

    def remote(src, dst, send, recv, device):
        return pltpu.make_async_remote_copy(
            src_ref=src,
            dst_ref=dst,
            send_sem=send,
            recv_sem=recv,
            device_id=device,
            device_id_type=MESH,
        )

    def state_span(s):
        return pl.ds(s * state_rows, state_rows)

    def state_copy(i, s):
        number = i * STATE_PIECES + s
        return remote(
            state.at[(1 - side) * half + i, state_span(s)],
            pair_state.at[i, state_span(s)],
            state_send.at[0, number],
            state_recv.at[0, number],
            {"seq": other},
        )

    def line_copy(b, i, s, first=False):
        number = i * STATE_PIECES + s
        return remote(
            (block if first else line_state).at[b, i, state_span(s)],
            line_state.at[b, i, state_span(s)],
            state_send.at[1 + b, number],
            state_recv.at[1 + b, number],
            {"seq": above},
        )

    def give_copy(i, s):
        number = i * STATE_PIECES + s
        return remote(
            give.at[i, state_span(s)],
            mix.at[side * half + i, state_span(s)],
            state_send.at[1 + line_bits, number],
            state_recv.at[1 + line_bits, number],
            {"seq": other},
        )

    def token_span(h):
        return pl.ds(pl.multiple_of(h * token_share, token_share), token_share)

    def grad_copy(p):
        return remote(
            quarter.at[slots(p)],
            theirs.at[slots(p), :, token_span(head)],
            grad_send.at[0, p],
            grad_recv.at[0, p],
            {"seq": other},
        )

    def share_copy(r, bit, p):
        owned = theirs.at[slots(p), :, token_span(flip(head, r))]
        slot = r ^ (1 << bit)
        return remote(
            owned,
            owned,
            grad_send.at[slot, p],
            grad_recv.at[slot, p],
            {"head": flip(head, 1 << bit)},
        )

    def square_copy(r):
        away = r >= heads
        return remote(
            squares.at[pl.ds(0, 1)],
            squares_in.at[r, pl.ds(0, 1)],
            square_send.at[r],
            square_recv.at[r],
            {"seq": other if away else me, "head": flip(head, r % heads)},
        )

    def pair_copy(k, t):
        at = pl.ds(t * (tokens // 2), tokens // 2)
        return remote(
            raw.at[k, at],
            came.at[k, at],
            pair_send.at[k, t],
            pair_recv.at[k, t],
            {"seq": other},
        )

    def part_span(q):
        return pl.ds(q * part_rows, part_rows)

    def up_copy(k, d, q):
        return remote(
            part.at[k, d, part_span(q)],
            rising.at[k, d, part_span(q)],
            up_send.at[k, d, q],
            up_recv.at[k, d, q],
            {"seq": above},
        )

    def down_copy(k, d, q):
        return remote(
            part.at[k, d, part_span(q)],
            falling.at[k, d, part_span(q)],
            down_send.at[k, d, q],
            down_recv.at[k, d, q],
            {"seq": below},
        )

    copies[0].wait()
    copies[1].wait()
    for i in range(half):
        h = (1 - side) * half + i
        state[h] = matmul(k_ref[:, columns(h)], v_ref[:, columns(h)], TN)
        if i == 0:
            peers = 2 * heads - 1 + jnp.where(place > 0, 1, 0) + jnp.where(place < line - 1, 1, 0)
            pl.semaphore_wait(barrier, peers)
        for s in range(STATE_PIECES):
            state_copy(i, s).start()
    for i in range(half):
        h = side * half + i
        state[h] = matmul(k_ref[:, columns(h)], v_ref[:, columns(h)], TN)

    copies[2].wait()
    tile = max(rows, lanes)
    for j in range(grad_ref.shape[1] // tile):
        flat = grad_ref[:, j * tile : (j + 1) * tile].T
        for i in range(tile // rows):
            owner = j * (tile // rows) + i
            turned[owner % 2, owner // 2] = flat[i * rows : (i + 1) * rows]
    quarter[...] = turned[1 - side, :, :, token_span(head)].astype(jnp.float32)
    for p in range(last):
        grad_copy(p).start()

    def forward(i, p):
        for r in held[i]:
            share_copy(r, stages[i], p).start()

    def collect(i, p):
        for r in held[i]:
            share_copy(r, stages[i], p).wait_recv()

    def pass_on(p):
        grad_copy(p).wait_recv()
        forward(0, p)

    def near(h):
        weight = scale * level_ref[h, 0].astype(jnp.float32)
        scores = matmul(q_ref[:, span(h)], k_ref[:, span(h)], NT) * weight
        row = lax.broadcasted_iota(jnp.int32, scores.shape, 0)
        column = lax.broadcasted_iota(jnp.int32, scores.shape, 1)
        probs = jnp.where(column <= row, scores, 0.0).astype(jnp.bfloat16)
        raw[h] = matmul(probs, v_ref[:, span(h)])

    def level(i, number):
        return level_ref[side * half + i, number].astype(jnp.float32)

    for b in range(line_bits):

        @pl.when(bit_of(b) == 0)
        def _():
            line_state[b] = jnp.zeros(line_state.shape[1:], jnp.float32)

    copies[3].wait()
    for i, s in state_parts:
        at = (i, state_span(s))
        state_copy(i, s).wait_recv()
        block[0, *at] = state[side * half + i, state_span(s)] + pair_state[*at]

        @pl.when(bit_of(0) == 0)
        def _():
            line_copy(0, i, s, True).start()

    @pl.when(high_end)
    def _():
        for h in range(chunks):
            near(h)
        pass_on(0)

    for i, s in state_parts:
        at = (i, state_span(s))
        for b in range(line_bits):

            @pl.when(bit_of(b) == 1)
            def _():
                line_copy(b, i, s).wait_recv()

            if b:

                @pl.when(jnp.logical_and(bit_of(b) == 1, jnp.logical_not(ends_block(b))))
                def _():
                    line_copy(b, i, s).start()

            if b + 1 < line_bits:
                block[b + 1, *at] = block[b, *at] + line_state[b, *at]

                @pl.when(jnp.logical_and(bit_of(b + 1) == 0, ends_block(b + 1)))
                def _():
                    line_copy(b + 1, i, s, True).start()

        far = jnp.zeros((state_rows, lanes), jnp.float32)
        for b in range(line_bits):
            far = far + (level(i, 2 + b) * bit_of(b).astype(jnp.float32)) * line_state[b, *at]
        first = level(i, 1)
        right = side.astype(jnp.float32)
        mix[side * half + i, state_span(s)] = far + (first * right) * pair_state[*at]
        give[*at] = far + (first * (1.0 - right)) * state[side * half + i, state_span(s)]
        give_copy(i, s).start()

    @pl.when(jnp.logical_not(high_end))
    def _():
        for h in range(chunks):
            near(h)
            if h == 0:
                pass_on(0)

    for p in range(1, last):
        pass_on(p)

    total = jnp.zeros((tokens, lanes), jnp.float32)
    for h in range(chunks):

        @pl.when(side != h // half)
        def _():
            for s in range(STATE_PIECES):
                give_copy(h % half, s).wait_recv()

        high, low = split(mix[h])
        query = q_ref[:, span(h)]
        value = raw[h] + scale * (matmul(query, high) + matmul(query, low))
        raw[h] = value
        if h == 0:
            pair_copy(0, 0).start()
        total = total + value * value
    ones = jnp.ones((8, lanes), jnp.bfloat16)
    high, low = split(total)
    squares[...] = matmul(ones, high, NT) + matmul(ones, low, NT)
    for r in range(1, 2 * heads):
        square_copy(r).start()
    pair_copy(0, 1).start()
    for p in range(last):
        collect(0, p)
        for i in range(1, head_bits):
            if i > 1:
                collect(i - 1, p)
            forward(i, p)
    for t in range(2):
        pair_copy(1, t).start()
    grad_copy(last).start()
    for k in range(2, chunks):
        for t in range(2):
            pair_copy(k, t).start()

    def inverse_of(whole):
        root = lax.rsqrt(whole / D + 1e-06)
        return jnp.broadcast_to(root, (8, tokens)).T[:, :1]

    whole = squares[0:1]
    for r in range(1, heads):
        square_copy(r).wait_recv()
        whole = whole + squares_in[r, 0:1]
    inverse = inverse_of(whole)
    for h in range(chunks):
        normed_ref[:, span(h)] = (raw[h] * inverse).astype(jnp.bfloat16)

    def arrive(p):
        collect(head_bits - 1, p)
        theirs_half[slots(p)] = theirs[slots(p)].astype(jnp.bfloat16)

    for p in range(last):
        arrive(p)

    def product(k, p):
        flat = (group * rows, tokens)
        value = matmul(turned[side, slots(p)].reshape(flat), normed_ref[:, span(k)])
        value = value + matmul(theirs_half[slots(p)].reshape(flat), there[k])
        part[k, slots(p)] = value.reshape(group, rows, lanes)
        start = first_slot(p)

        @pl.when(high_end)
        def _():
            @pl.loop(0, group)
            def _(i):
                @pl.when(start + i < place)
                def _():
                    for q in range(SLOT_PIECES):
                        down_copy(k, start + i, q).start()

        @pl.when(low_end)
        def _():
            @pl.loop(0, group)
            def _(i):
                @pl.when(start + i > place)
                def _():
                    for q in range(SLOT_PIECES):
                        up_copy(k, start + i, q).start()

    def rise(k):
        @pl.loop(0, line - 1 - place)
        def _(i):
            d = line - 1 - i
            for q in range(SLOT_PIECES):
                up_copy(k, d, q).wait_recv()
                part[k, d, part_span(q)] = part[k, d, part_span(q)] + rising[k, d, part_span(q)]
                up_copy(k, d, q).start()

    def fall(k):
        @pl.loop(0, place)
        def _(d):
            for q in range(SLOT_PIECES):
                down_copy(k, d, q).wait_recv()
                part[k, d, part_span(q)] = part[k, d, part_span(q)] + falling[k, d, part_span(q)]
                down_copy(k, d, q).start()

    inner = jnp.logical_and(place > 0, place < line - 1)

    def nearer(k):
        @pl.when(jnp.logical_and(inner, lower))
        def _():
            rise(k)

        @pl.when(jnp.logical_and(inner, jnp.logical_not(lower)))
        def _():
            fall(k)

    def farther(k):
        @pl.when(jnp.logical_and(inner, lower))
        def _():
            fall(k)

        @pl.when(jnp.logical_and(inner, jnp.logical_not(lower)))
        def _():
            rise(k)

    alone = group == 1
    whole = jnp.zeros((1, tokens), jnp.float32)
    for r in range(heads, 2 * heads):
        square_copy(r).wait_recv()
        whole = whole + squares_in[r, 0:1]
    their_inverse = inverse_of(whole)
    for k in range(chunks):
        for t in range(2):
            pair_copy(k, t).wait_recv()
        there[k] = (came[k] * their_inverse).astype(jnp.bfloat16)
        for p in range(last):
            product(k, p)
        if k == 0 and alone:
            nearer(0)
        if k == 1:
            if alone:
                farther(0)
            pass_on(last)
            collect(0, last)
            for i in range(1, head_bits):
                if i > 1:
                    collect(i - 1, last)
                forward(i, last)
            arrive(last)
            product(0, last)
            product(1, last)
            if not alone:
                nearer(0)
                farther(0)
        if k > 1:
            product(k, last)
            nearer(k - 1)
            farther(k - 1)
    nearer(chunks - 1)
    farther(chunks - 1)

    for i, s in state_parts:
        state_copy(i, s).wait_send()
        for b in range(line_bits):

            @pl.when(jnp.logical_xor(bit_of(b) == 1, ends_block(b)))
            def _():
                line_copy(b, i, s).wait_send()

        give_copy(i, s).wait_send()
    for p in range(PIECES):
        grad_copy(p).wait_send()
        for i in range(head_bits):
            for r in held[i]:
                share_copy(r, stages[i], p).wait_send()
    for r in range(1, 2 * heads):
        square_copy(r).wait_send()
    for k in range(chunks):
        for t in range(2):
            pair_copy(k, t).wait_send()

    def settle(k):
        for q in range(SLOT_PIECES):

            @pl.loop(place + 1, line)
            def _(d):
                up_copy(k, d, q).wait_send()

            @pl.loop(0, place)
            def _(d):
                down_copy(k, d, q).wait_send()

    for k in range(chunks):
        if k:
            settle(k - 1)
        out_ref[:, span(k)] = part[k, place]

        @pl.when(place > 0)
        def _():
            for q in range(SLOT_PIECES):
                up_copy(k, place, q).wait_recv()
            out_ref[:, span(k)] = out_ref[:, span(k)] + rising[k, place]

        @pl.when(place < line - 1)
        def _():
            for q in range(SLOT_PIECES):
                down_copy(k, place, q).wait_recv()
            out_ref[:, span(k)] = out_ref[:, span(k)] + falling[k, place]

    settle(chunks - 1)


def body(queries, keys, values, level_weights, out_grad):
    tokens, width = queries.shape
    assert tokens == GROUP
    count = lax.axis_size("seq")
    heads = lax.axis_size("head")
    line = count // 2
    line_bits = line.bit_length() - 1
    lanes = D // HEADS
    chunks = width // lanes
    half = chunks // 2
    rows = out_grad.shape[1] // count
    slots = (chunks, line, rows, lanes)
    states = (half, lanes, lanes)
    vmem = pl.BlockSpec(memory_space=pltpu.VMEM)
    smem = pl.BlockSpec(memory_space=pltpu.SMEM)
    away = pl.BlockSpec(memory_space=pltpu.MemorySpace.HBM)
    f32 = jnp.float32
    dma = pltpu.SemaphoreType.DMA
    return pl.pallas_call(
        functools.partial(kernel, line, heads),
        out_shape=(
            pltpu.VMEM((tokens, width), jnp.bfloat16),
            pltpu.VMEM((rows, width), f32),
        ),
        in_specs=[away, away, away, smem, away],
        out_specs=(vmem, vmem),
        scratch_shapes=[
            pltpu.VMEM(queries.shape, queries.dtype),
            pltpu.VMEM(keys.shape, keys.dtype),
            pltpu.VMEM(values.shape, values.dtype),
            pltpu.VMEM(out_grad.shape, out_grad.dtype),
            pltpu.SemaphoreType.DMA((4,)),
            pltpu.VMEM((chunks, lanes, lanes), f32),
            pltpu.VMEM(states, f32),
            pltpu.VMEM((line_bits, *states), f32),
            pltpu.VMEM((line_bits, *states), f32),
            pltpu.VMEM(states, f32),
            pltpu.VMEM((chunks, lanes, lanes), f32),
            pltpu.VMEM((2, line, rows, tokens), jnp.bfloat16),
            pltpu.VMEM((line, rows, tokens // heads), f32),
            pltpu.VMEM((line, rows, tokens), f32),
            pltpu.VMEM((line, rows, tokens), jnp.bfloat16),
            pltpu.VMEM((chunks, tokens, lanes), f32),
            pltpu.VMEM((chunks, tokens, lanes), f32),
            pltpu.VMEM((chunks, tokens, lanes), jnp.bfloat16),
            pltpu.VMEM((8, tokens), f32),
            pltpu.VMEM((2 * heads, 8, tokens), f32),
            pltpu.VMEM(slots, f32),
            pltpu.VMEM(slots, f32),
            pltpu.VMEM(slots, f32),
            dma((2 + line_bits, half * STATE_PIECES)),
            dma((2 + line_bits, half * STATE_PIECES)),
            dma((heads, PIECES)),
            dma((heads, PIECES)),
            dma((2 * heads,)),
            dma((2 * heads,)),
            dma((chunks, 2)),
            dma((chunks, 2)),
            dma((chunks, line, SLOT_PIECES)),
            dma((chunks, line, SLOT_PIECES)),
            dma((chunks, line, SLOT_PIECES)),
            dma((chunks, line, SLOT_PIECES)),
        ],
        compiler_params=pltpu.CompilerParams(
            collective_id=0, has_side_effects=True, vmem_limit_bytes=60 << 20
        ),
    )(queries, keys, values, level_weights, out_grad)


def solution(mesh):
    return jax.shard_map(
        body,
        mesh=mesh,
        in_specs=(
            P("seq", "head"),
            P("seq", "head"),
            P("seq", "head"),
            P("head", None),
            P("seq", None),
        ),
        out_specs=(P("seq", "head"), P("seq", "head")),
        check_vma=False,
    )
```

```python
import functools

import jax
import jax.numpy as jnp
from jax import lax
from jax.experimental import pallas as pl
from jax.experimental.pallas import tpu as pltpu
from jax.sharding import PartitionSpec as P

D = 2048
HEADS = 16
GROUP = 512
PIECES = 4
STATE_PIECES = 2
FIRST_SLOT_PIECES = 1
SLOT_PIECES = 2
MESH = pl.DeviceIdType.MESH
NT = (((1,), (1,)), ((), ()))
TN = (((0,), (0,)), ((), ()))


def flip(index, mask):
    bit = 1
    while bit <= mask:
        if mask & bit:
            index = index + bit - 2 * bit * ((index // bit) % 2)
        bit *= 2
    return index


def matmul(a, b, dims=(((1,), (0,)), ((), ()))):
    return lax.dot_general(a, b, dims, preferred_element_type=jnp.float32)


def split(x):
    high = x.astype(jnp.bfloat16)
    return high, (x - high.astype(jnp.float32)).astype(jnp.bfloat16)


def kernel(
    line,
    heads,
    q_in,
    k_in,
    v_in,
    level_in,
    grad_in,
    normed_ref,
    out_ref,
    q_ref,
    k_ref,
    v_ref,
    grad_ref,
    level_ref,
    loads,
    state,
    pair_state,
    block,
    line_state,
    give,
    mix,
    turned,
    quarter,
    theirs,
    theirs_half,
    raw,
    came,
    there,
    squares,
    squares_in,
    part,
    rising,
    falling,
    state_send,
    state_recv,
    grad_send,
    grad_recv,
    square_send,
    square_recv,
    pair_send,
    pair_recv,
    slot_send,
    slot_recv,
):
    me = lax.axis_index("seq")
    head = lax.axis_index("head")
    place = me // 2
    side = me % 2
    other = flip(me, 1)
    above = me + 2
    below = me - 2
    tokens, width = q_ref.shape
    lanes = D // HEADS
    chunks = width // lanes
    half = chunks // 2
    rows = out_ref.shape[0]
    line_bits = line.bit_length() - 1
    head_bits = heads.bit_length() - 1
    group = line // PIECES
    last = PIECES - 1
    bulk = [(p, 0, rows) for p in range(last - 1)]
    bulk += [(last - 1, 0, rows // 2), (last - 1, rows // 2, rows // 2)]
    bulk += [(last, 0, rows)]
    late, final = len(bulk) - 2, len(bulk) - 1
    token_share = tokens // heads
    state_rows = lanes // STATE_PIECES
    stages = list(reversed(range(head_bits)))
    held = [[0]]
    for bit in stages:
        held.append(held[-1] + [r ^ (1 << bit) for r in held[-1]])
    state_parts = [(i, s) for i in range(half) for s in range(STATE_PIECES)]
    scale = lanes ** (-0.5)
    low_end = place == 0
    high_end = place == line - 1

    def span(k):
        return slice(k * lanes, (k + 1) * lanes)

    def columns(k):
        return pl.ds(pl.multiple_of(k * lanes, lanes), lanes)

    def bit_of(b):
        return (place // (1 << b)) % 2

    def ends_block(b):
        return place % (1 << b) == (1 << b) - 1

    mine = place // group
    lower = place < line // 2

    def first_slot(p):
        ordered = jnp.where(lower, mine + PIECES - 1 - p, mine + 1 + p)
        return (ordered % PIECES) * group

    def slots(p):
        return pl.ds(first_slot(p), group)

    pairs = ((k_in, k_ref), (v_in, v_ref), (grad_in, grad_ref), (q_in, q_ref), (level_in, level_ref))
    copies = [pltpu.make_async_copy(a, b, loads.at[i]) for i, (a, b) in enumerate(pairs)]
    for copy in copies:
        copy.start()

    barrier = pltpu.get_barrier_semaphore()

    def greet(device):
        pl.semaphore_signal(barrier, inc=1, device_id=device, device_id_type=MESH)

    greet({"seq": other})
    for r in range(1, heads):
        greet({"head": flip(head, r)})
        greet({"seq": other, "head": flip(head, r)})

    @pl.when(place < line - 1)
    def _():
        greet({"seq": above})

    @pl.when(place > 0)
    def _():
        greet({"seq": below})

    def remote(src, dst, send, recv, device):
        return pltpu.make_async_remote_copy(
            src_ref=src,
            dst_ref=dst,
            send_sem=send,
            recv_sem=recv,
            device_id=device,
            device_id_type=MESH,
        )

    def state_span(s):
        return pl.ds(s * state_rows, state_rows)

    def state_copy(i, s):
        number = i * STATE_PIECES + s
        return remote(
            state.at[(1 - side) * half + i, state_span(s)],
            pair_state.at[i, state_span(s)],
            state_send.at[0],
            state_recv.at[0, number],
            {"seq": other},
        )

    def line_copy(b, i, s, first=False):
        number = i * STATE_PIECES + s
        return remote(
            (block if first else line_state).at[b, i, state_span(s)],
            line_state.at[b, i, state_span(s)],
            state_send.at[1 + b],
            state_recv.at[1 + b, number],
            {"seq": above},
        )

    def give_copy(i, s):
        number = i * STATE_PIECES + s
        return remote(
            give.at[i, state_span(s)],
            mix.at[side * half + i, state_span(s)],
            state_send.at[1 + line_bits],
            state_recv.at[1 + line_bits, number],
            {"seq": other},
        )

    def token_span(h):
        return pl.ds(pl.multiple_of(h * token_share, token_share), token_share)

    def grad_copy(e):
        p, start, size = bulk[e]
        return remote(
            quarter.at[slots(p), pl.ds(start, size)],
            theirs.at[slots(p), pl.ds(start, size), token_span(head)],
            grad_send.at[0],
            grad_recv.at[0, e],
            {"seq": other},
        )

    def share_copy(r, bit, e):
        p, start, size = bulk[e]
        owned = theirs.at[slots(p), pl.ds(start, size), token_span(flip(head, r))]
        slot = r ^ (1 << bit)
        return remote(
            owned,
            owned,
            grad_send.at[0],
            grad_recv.at[slot, e],
            {"head": flip(head, 1 << bit)},
        )

    def square_copy(r):
        away = r >= heads
        return remote(
            squares.at[pl.ds(0, 1)],
            squares_in.at[r, pl.ds(0, 1)],
            square_send.at[0],
            square_recv.at[r],
            {"seq": other if away else me, "head": flip(head, r % heads)},
        )

    def pair_copy(k, t):
        size = tokens // pair_parts(k)
        at = pl.ds(t * size, size)
        return remote(
            raw.at[k, at],
            came.at[k, at],
            pair_send.at[0],
            pair_recv.at[k + 1 if k else t],
            {"seq": other},
        )

    def pair_parts(k):
        return 1 if k else 2

    def slot_parts(k):
        return SLOT_PIECES if k == chunks - 1 else FIRST_SLOT_PIECES

    def part_span(k, q):
        size = rows // slot_parts(k)
        return pl.ds(q * size, size)

    def lane_of(k, q):
        return k * FIRST_SLOT_PIECES + q

    def up_copy(k, d, q):
        return remote(
            part.at[k, d, part_span(k, q)],
            rising.at[k, d, part_span(k, q)],
            slot_send.at[0],
            slot_recv.at[lane_of(k, q), d],
            {"seq": above},
        )

    def down_copy(k, d, q):
        return remote(
            part.at[k, d, part_span(k, q)],
            falling.at[k, d, part_span(k, q)],
            slot_send.at[0],
            slot_recv.at[lane_of(k, q), (d + line) % (line + 1)],
            {"seq": below},
        )

    copies[0].wait()
    copies[1].wait()
    for i in range(half):
        h = (1 - side) * half + i
        state[h] = matmul(k_ref[:, columns(h)], v_ref[:, columns(h)], TN)
        if i == 0:
            peers = 2 * heads - 1 + jnp.where(place > 0, 1, 0) + jnp.where(place < line - 1, 1, 0)
            pl.semaphore_wait(barrier, peers)
        for s in range(STATE_PIECES):
            state_copy(i, s).start()
    for i in range(half):
        h = side * half + i
        state[h] = matmul(k_ref[:, columns(h)], v_ref[:, columns(h)], TN)

    copies[2].wait()
    tile = max(rows, lanes)
    for j in range(grad_ref.shape[1] // tile):
        flat = grad_ref[:, j * tile : (j + 1) * tile].T
        for i in range(tile // rows):
            owner = j * (tile // rows) + i
            turned[owner % 2, owner // 2] = flat[i * rows : (i + 1) * rows]
    quarter[...] = turned[1 - side, :, :, token_span(head)].astype(jnp.float32)
    for e in range(late):
        grad_copy(e).start()

    def forward(i, p):
        for r in held[i]:
            share_copy(r, stages[i], p).start()

    def collect(i, p):
        for r in held[i]:
            share_copy(r, stages[i], p).wait_recv()

    def pass_on(p):
        grad_copy(p).wait_recv()
        forward(0, p)

    def near(h):
        weight = scale * level_ref[h, 0].astype(jnp.float32)
        scores = matmul(q_ref[:, span(h)], k_ref[:, span(h)], NT) * weight
        row = lax.broadcasted_iota(jnp.int32, scores.shape, 0)
        column = lax.broadcasted_iota(jnp.int32, scores.shape, 1)
        probs = jnp.where(column <= row, scores, 0.0).astype(jnp.bfloat16)
        raw[h] = matmul(probs, v_ref[:, span(h)])

    def level(i, number):
        return level_ref[side * half + i, number].astype(jnp.float32)

    for b in range(line_bits):

        @pl.when(bit_of(b) == 0)
        def _():
            line_state[b] = jnp.zeros(line_state.shape[1:], jnp.float32)

    copies[3].wait()
    copies[4].wait()
    for i, s in state_parts:
        at = (i, state_span(s))
        state_copy(i, s).wait_recv()
        block[0, *at] = state[side * half + i, state_span(s)] + pair_state[*at]

        @pl.when(bit_of(0) == 0)
        def _():
            line_copy(0, i, s, True).start()

    @pl.when(high_end)
    def _():
        for h in range(chunks):
            near(h)
        pass_on(0)

    for i, s in state_parts:
        at = (i, state_span(s))
        for b in range(line_bits):

            @pl.when(bit_of(b) == 1)
            def _():
                line_copy(b, i, s).wait_recv()

            if b:

                @pl.when(jnp.logical_and(bit_of(b) == 1, jnp.logical_not(ends_block(b))))
                def _():
                    line_copy(b, i, s).start()

            if b + 1 < line_bits:
                block[b + 1, *at] = block[b, *at] + line_state[b, *at]

                @pl.when(jnp.logical_and(bit_of(b + 1) == 0, ends_block(b + 1)))
                def _():
                    line_copy(b + 1, i, s, True).start()

        far = jnp.zeros((state_rows, lanes), jnp.float32)
        for b in range(line_bits):
            far = far + (level(i, 2 + b) * bit_of(b).astype(jnp.float32)) * line_state[b, *at]
        first = level(i, 1)
        right = side.astype(jnp.float32)
        mix[side * half + i, state_span(s)] = far + (first * right) * pair_state[*at]
        give[*at] = far + (first * (1.0 - right)) * state[side * half + i, state_span(s)]
        give_copy(i, s).start()

    grad_copy(late).start()

    @pl.when(jnp.logical_not(high_end))
    def _():
        for h in range(chunks):
            near(h)
            if h == 0:
                pass_on(0)

    for e in range(1, late):
        pass_on(e)

    total = jnp.zeros((tokens, lanes), jnp.float32)
    for h in range(chunks):

        @pl.when(side != h // half)
        def _():
            for s in range(STATE_PIECES):
                give_copy(h % half, s).wait_recv()

        high, low = split(mix[h])
        query = q_ref[:, span(h)]
        value = raw[h] + scale * (matmul(query, high) + matmul(query, low))
        raw[h] = value
        if h == 0:
            pair_copy(0, 0).start()
        total = total + value * value
    ones = jnp.ones((8, lanes), jnp.bfloat16)
    high, low = split(total)
    squares[...] = matmul(ones, high, NT) + matmul(ones, low, NT)
    for r in range(1, 2 * heads):
        square_copy(r).start()
    pair_copy(0, 1).start()
    pass_on(late)
    for e in range(final):
        collect(0, e)
        for i in range(1, head_bits):
            if i > 1:
                collect(i - 1, e)
            forward(i, e)
    pair_copy(1, 0).start()
    grad_copy(final).start()
    for k in range(2, chunks):
        pair_copy(k, 0).start()

    def inverse_of(whole):
        root = lax.rsqrt(whole / D + 1e-06)
        return jnp.broadcast_to(root, (8, tokens)).T[:, :1]

    whole = squares[0:1]
    for r in range(1, heads):
        square_copy(r).wait_recv()
        whole = whole + squares_in[r, 0:1]
    inverse = inverse_of(whole)
    for h in range(chunks):
        normed_ref[:, span(h)] = (raw[h] * inverse).astype(jnp.bfloat16)

    def arrive(p):
        for e in range(len(bulk)):
            if bulk[e][0] == p:
                collect(head_bits - 1, e)
        theirs_half[slots(p)] = theirs[slots(p)].astype(jnp.bfloat16)

    for p in range(last):
        arrive(p)

    def product(k, p):
        flat = (group * rows, tokens)
        value = matmul(turned[side, slots(p)].reshape(flat), normed_ref[:, span(k)])
        value = value + matmul(theirs_half[slots(p)].reshape(flat), there[k])
        part[k, slots(p)] = value.reshape(group, rows, lanes)
        start = first_slot(p)

        @pl.when(high_end)
        def _():
            @pl.loop(0, group)
            def _(i):
                @pl.when(start + i < place)
                def _():
                    for q in range(slot_parts(k)):
                        down_copy(k, start + i, q).start()

        @pl.when(low_end)
        def _():
            @pl.loop(0, group)
            def _(i):
                @pl.when(start + i > place)
                def _():
                    for q in range(slot_parts(k)):
                        up_copy(k, start + i, q).start()

    def rise(k):
        @pl.loop(0, line - 1 - place)
        def _(i):
            d = line - 1 - i
            for q in range(slot_parts(k)):
                up_copy(k, d, q).wait_recv()
                part[k, d, part_span(k, q)] = part[k, d, part_span(k, q)] + rising[k, d, part_span(k, q)]
                up_copy(k, d, q).start()

    def fall(k):
        @pl.loop(0, place)
        def _(d):
            for q in range(slot_parts(k)):
                down_copy(k, d, q).wait_recv()
                part[k, d, part_span(k, q)] = part[k, d, part_span(k, q)] + falling[k, d, part_span(k, q)]
                down_copy(k, d, q).start()

    inner = jnp.logical_and(place > 0, place < line - 1)

    def nearer(k):
        @pl.when(jnp.logical_and(inner, lower))
        def _():
            rise(k)

        @pl.when(jnp.logical_and(inner, jnp.logical_not(lower)))
        def _():
            fall(k)

    def farther(k):
        @pl.when(jnp.logical_and(inner, lower))
        def _():
            fall(k)

        @pl.when(jnp.logical_and(inner, jnp.logical_not(lower)))
        def _():
            rise(k)

    alone = group == 1
    whole = jnp.zeros((1, tokens), jnp.float32)
    for r in range(heads, 2 * heads):
        square_copy(r).wait_recv()
        whole = whole + squares_in[r, 0:1]
    their_inverse = inverse_of(whole)
    for k in range(chunks):
        for t in range(pair_parts(k)):
            pair_copy(k, t).wait_recv()
        there[k] = (came[k] * their_inverse).astype(jnp.bfloat16)
        for p in range(last):
            product(k, p)
        if k == 0 and alone:
            nearer(0)
        if k == 1:
            if alone:
                farther(0)
            pass_on(final)
            collect(0, final)
            for i in range(1, head_bits):
                if i > 1:
                    collect(i - 1, final)
                forward(i, final)
            arrive(last)
            product(0, last)
            product(1, last)
            if not alone:
                nearer(0)
                farther(0)
        if k > 1:
            product(k, last)
            nearer(k - 1)
            farther(k - 1)
    nearer(chunks - 1)
    farther(chunks - 1)

    def drain(ref, sem):
        remote(ref, ref, sem, sem, {"seq": other}).wait_send()

    drain(pair_state, state_send.at[0])
    for b in range(line_bits):

        @pl.when(jnp.logical_xor(bit_of(b) == 1, ends_block(b)))
        def _():
            drain(block.at[b], state_send.at[1 + b])

    drain(give, state_send.at[1 + line_bits])
    drain(theirs, grad_send.at[0])
    drain(squares_in.at[pl.ds(1, 2 * heads - 1), pl.ds(0, 1)], square_send.at[0])
    drain(raw, pair_send.at[0])

    for k in range(chunks):
        out_ref[:, span(k)] = part[k, place]

        @pl.when(place > 0)
        def _():
            for q in range(slot_parts(k)):
                up_copy(k, place, q).wait_recv()
            out_ref[:, span(k)] = out_ref[:, span(k)] + rising[k, place]

        @pl.when(place < line - 1)
        def _():
            for q in range(slot_parts(k)):
                down_copy(k, place, q).wait_recv()
            out_ref[:, span(k)] = out_ref[:, span(k)] + falling[k, place]

    drain(part.at[:, pl.ds(0, line - 1)], slot_send.at[0])


def body(queries, keys, values, level_weights, out_grad):
    tokens, width = queries.shape
    assert tokens == GROUP
    count = lax.axis_size("seq")
    heads = lax.axis_size("head")
    line = count // 2
    line_bits = line.bit_length() - 1
    lanes = D // HEADS
    chunks = width // lanes
    half = chunks // 2
    rows = out_grad.shape[1] // count
    slots = (chunks, line, rows, lanes)
    states = (half, lanes, lanes)
    vmem = pl.BlockSpec(memory_space=pltpu.VMEM)
    away = pl.BlockSpec(memory_space=pltpu.MemorySpace.HBM)
    f32 = jnp.float32
    dma = pltpu.SemaphoreType.DMA
    return pl.pallas_call(
        functools.partial(kernel, line, heads),
        out_shape=(
            pltpu.VMEM((tokens, width), jnp.bfloat16),
            pltpu.VMEM((rows, width), f32),
        ),
        in_specs=[away] * 5,
        out_specs=(vmem, vmem),
        scratch_shapes=[
            pltpu.VMEM(queries.shape, queries.dtype),
            pltpu.VMEM(keys.shape, keys.dtype),
            pltpu.VMEM(values.shape, values.dtype),
            pltpu.VMEM(out_grad.shape, out_grad.dtype),
            pltpu.SMEM(level_weights.shape, level_weights.dtype),
            dma((5,)),
            pltpu.VMEM((chunks, lanes, lanes), f32),
            pltpu.VMEM(states, f32),
            pltpu.VMEM((line_bits, *states), f32),
            pltpu.VMEM((line_bits, *states), f32),
            pltpu.VMEM(states, f32),
            pltpu.VMEM((chunks, lanes, lanes), f32),
            pltpu.VMEM((2, line, rows, tokens), jnp.bfloat16),
            pltpu.VMEM((line, rows, tokens // heads), f32),
            pltpu.VMEM((line, rows, tokens), f32),
            pltpu.VMEM((line, rows, tokens), jnp.bfloat16),
            pltpu.VMEM((chunks, tokens, lanes), f32),
            pltpu.VMEM((chunks, tokens, lanes), f32),
            pltpu.VMEM((chunks, tokens, lanes), jnp.bfloat16),
            pltpu.VMEM((8, tokens), f32),
            pltpu.VMEM((2 * heads, 8, tokens), f32),
            pltpu.VMEM(slots, f32),
            pltpu.VMEM(slots, f32),
            pltpu.VMEM(slots, f32),
            dma((2 + line_bits,)),
            dma((2 + line_bits, half * STATE_PIECES)),
            dma((1,)),
            dma((heads, PIECES + 1)),
            dma((1,)),
            dma((2 * heads,)),
            dma((1,)),
            dma((chunks + 1,)),
            dma((1,)),
            dma(((chunks - 1) * FIRST_SLOT_PIECES + SLOT_PIECES, line + 1)),
        ],
        compiler_params=pltpu.CompilerParams(
            collective_id=0, has_side_effects=True, vmem_limit_bytes=60 << 20
        ),
    )(queries, keys, values, level_weights, out_grad)


def solution(mesh):
    return jax.shard_map(
        body,
        mesh=mesh,
        in_specs=(
            P("seq", "head"),
            P("seq", "head"),
            P("seq", "head"),
            P("head", None),
            P("seq", None),
        ),
        out_specs=(P("seq", "head"), P("seq", "head")),
        check_vma=False,
    )
```

```python
import functools

import jax
import jax.numpy as jnp
from jax import lax
from jax.experimental import pallas as pl
from jax.experimental.pallas import tpu as pltpu
from jax.sharding import PartitionSpec as P

D = 2048
HEADS = 16
GROUP = 512
PIECES = 4
STATE_PIECES = 2
FIRST_SLOT_PIECES = 1
SLOT_PIECES = 4
SUBLANES = 8
MESH = pl.DeviceIdType.MESH
NT = (((1,), (1,)), ((), ()))
TN = (((0,), (0,)), ((), ()))


def flip(index, mask):
    bit = 1
    while bit <= mask:
        if mask & bit:
            index = index + bit - 2 * bit * ((index // bit) % 2)
        bit *= 2
    return index


def matmul(a, b, dims=(((1,), (0,)), ((), ()))):
    return lax.dot_general(a, b, dims, preferred_element_type=jnp.float32)


def split(x):
    high = x.astype(jnp.bfloat16)
    return high, (x - high.astype(jnp.float32)).astype(jnp.bfloat16)


def last_parts(rows):
    return max(1, min(SLOT_PIECES, rows // SUBLANES))


def kernel(
    line,
    heads,
    q_in,
    k_in,
    v_in,
    level_in,
    grad_in,
    normed_ref,
    out_ref,
    q_ref,
    k_ref,
    v_ref,
    grad_ref,
    level_ref,
    loads,
    state,
    pair_state,
    block,
    line_state,
    give,
    mix,
    turned,
    quarter,
    theirs,
    theirs_half,
    raw,
    came,
    there,
    squares,
    squares_in,
    part,
    rising,
    falling,
    state_send,
    state_recv,
    grad_send,
    grad_recv,
    square_send,
    square_recv,
    pair_send,
    pair_recv,
    slot_send,
    slot_recv,
):
    me = lax.axis_index("seq")
    head = lax.axis_index("head")
    place = me // 2
    side = me % 2
    other = flip(me, 1)
    above = me + 2
    below = me - 2
    tokens, width = q_ref.shape
    lanes = D // HEADS
    chunks = width // lanes
    half = chunks // 2
    rows = out_ref.shape[0]
    line_bits = line.bit_length() - 1
    head_bits = heads.bit_length() - 1
    group = line // PIECES
    last = PIECES - 1
    bulk = [(p, 0, rows) for p in range(last - 1)]
    bulk += [(last - 1, 0, rows // 2), (last - 1, rows // 2, rows // 2)]
    bulk += [(last, 0, rows)]
    late, final = len(bulk) - 2, len(bulk) - 1
    token_share = tokens // heads
    state_rows = lanes // STATE_PIECES
    stages = list(reversed(range(head_bits)))
    held = [[0]]
    for bit in stages:
        held.append(held[-1] + [r ^ (1 << bit) for r in held[-1]])
    state_parts = [(i, s) for i in range(half) for s in range(STATE_PIECES)]
    scale = lanes ** (-0.5)
    low_end = place == 0
    high_end = place == line - 1

    def span(k):
        return slice(k * lanes, (k + 1) * lanes)

    def columns(k):
        return pl.ds(pl.multiple_of(k * lanes, lanes), lanes)

    def bit_of(b):
        return (place // (1 << b)) % 2

    def ends_block(b):
        return place % (1 << b) == (1 << b) - 1

    mine = place // group
    lower = place < line // 2

    def first_slot(p):
        ordered = jnp.where(lower, mine + PIECES - 1 - p, mine + 1 + p)
        return (ordered % PIECES) * group

    def slots(p):
        return pl.ds(first_slot(p), group)

    pairs = ((k_in, k_ref), (v_in, v_ref), (grad_in, grad_ref), (q_in, q_ref), (level_in, level_ref))
    copies = [pltpu.make_async_copy(a, b, loads.at[i]) for i, (a, b) in enumerate(pairs)]
    for copy in copies:
        copy.start()

    barrier = pltpu.get_barrier_semaphore()

    def greet(device):
        pl.semaphore_signal(barrier, inc=1, device_id=device, device_id_type=MESH)

    greet({"seq": other})
    for r in range(1, heads):
        greet({"head": flip(head, r)})
        greet({"seq": other, "head": flip(head, r)})

    @pl.when(place < line - 1)
    def _():
        greet({"seq": above})

    @pl.when(place > 0)
    def _():
        greet({"seq": below})

    def remote(src, dst, send, recv, device):
        return pltpu.make_async_remote_copy(
            src_ref=src,
            dst_ref=dst,
            send_sem=send,
            recv_sem=recv,
            device_id=device,
            device_id_type=MESH,
        )

    def state_span(s):
        return pl.ds(s * state_rows, state_rows)

    def state_copy(i, s):
        number = i * STATE_PIECES + s
        return remote(
            state.at[(1 - side) * half + i, state_span(s)],
            pair_state.at[i, state_span(s)],
            state_send.at[0],
            state_recv.at[0, number],
            {"seq": other},
        )

    def line_copy(b, i, s, first=False):
        number = i * STATE_PIECES + s
        return remote(
            (block if first else line_state).at[b, i, state_span(s)],
            line_state.at[b, i, state_span(s)],
            state_send.at[1 + b],
            state_recv.at[1 + b, number],
            {"seq": above},
        )

    def give_copy(i, s):
        number = i * STATE_PIECES + s
        return remote(
            give.at[i, state_span(s)],
            mix.at[side * half + i, state_span(s)],
            state_send.at[1 + line_bits],
            state_recv.at[1 + line_bits, number],
            {"seq": other},
        )

    def token_span(h):
        return pl.ds(pl.multiple_of(h * token_share, token_share), token_share)

    def grad_copy(e):
        p, start, size = bulk[e]
        return remote(
            quarter.at[slots(p), pl.ds(start, size)],
            theirs.at[slots(p), pl.ds(start, size), token_span(head)],
            grad_send.at[0],
            grad_recv.at[0, e],
            {"seq": other},
        )

    def share_copy(r, bit, e):
        p, start, size = bulk[e]
        owned = theirs.at[slots(p), pl.ds(start, size), token_span(flip(head, r))]
        slot = r ^ (1 << bit)
        return remote(
            owned,
            owned,
            grad_send.at[0],
            grad_recv.at[slot, e],
            {"head": flip(head, 1 << bit)},
        )

    def square_copy(r):
        away = r >= heads
        return remote(
            squares.at[pl.ds(0, 1)],
            squares_in.at[r, pl.ds(0, 1)],
            square_send.at[0],
            square_recv.at[r],
            {"seq": other if away else me, "head": flip(head, r % heads)},
        )

    def pair_copy(k, t):
        size = tokens // pair_parts(k)
        at = pl.ds(t * size, size)
        return remote(
            raw.at[k, at],
            came.at[k, at],
            pair_send.at[0],
            pair_recv.at[k + 1 if k else t],
            {"seq": other},
        )

    def pair_parts(k):
        return 1 if k else 2

    def slot_parts(k):
        return last_parts(rows) if k == chunks - 1 else FIRST_SLOT_PIECES

    def part_span(k, q):
        size = rows // slot_parts(k)
        return pl.ds(q * size, size)

    def lane_of(k, q):
        return k * FIRST_SLOT_PIECES + q

    def up_copy(k, d, q):
        return remote(
            part.at[k, d, part_span(k, q)],
            rising.at[k, d, part_span(k, q)],
            slot_send.at[0],
            slot_recv.at[lane_of(k, q), d],
            {"seq": above},
        )

    def down_copy(k, d, q):
        return remote(
            part.at[k, d, part_span(k, q)],
            falling.at[k, d, part_span(k, q)],
            slot_send.at[0],
            slot_recv.at[lane_of(k, q), (d + line) % (line + 1)],
            {"seq": below},
        )

    copies[0].wait()
    copies[1].wait()
    for i in range(half):
        h = (1 - side) * half + i
        state[h] = matmul(k_ref[:, columns(h)], v_ref[:, columns(h)], TN)
        if i == 0:
            peers = 2 * heads - 1 + jnp.where(place > 0, 1, 0) + jnp.where(place < line - 1, 1, 0)
            pl.semaphore_wait(barrier, peers)
        for s in range(STATE_PIECES):
            state_copy(i, s).start()
    for i in range(half):
        h = side * half + i
        state[h] = matmul(k_ref[:, columns(h)], v_ref[:, columns(h)], TN)

    copies[2].wait()
    tile = max(rows, lanes)
    for j in range(grad_ref.shape[1] // tile):
        flat = grad_ref[:, j * tile : (j + 1) * tile].T
        for i in range(tile // rows):
            owner = j * (tile // rows) + i
            turned[owner % 2, owner // 2] = flat[i * rows : (i + 1) * rows]
    quarter[...] = turned[1 - side, :, :, token_span(head)].astype(jnp.float32)
    for e in range(late):
        grad_copy(e).start()

    def forward(i, p):
        for r in held[i]:
            share_copy(r, stages[i], p).start()

    def collect(i, p):
        for r in held[i]:
            share_copy(r, stages[i], p).wait_recv()

    def pass_on(p):
        grad_copy(p).wait_recv()
        forward(0, p)

    def near(h):
        weight = scale * level_ref[h, 0].astype(jnp.float32)
        scores = matmul(q_ref[:, span(h)], k_ref[:, span(h)], NT) * weight
        row = lax.broadcasted_iota(jnp.int32, scores.shape, 0)
        column = lax.broadcasted_iota(jnp.int32, scores.shape, 1)
        probs = jnp.where(column <= row, scores, 0.0).astype(jnp.bfloat16)
        raw[h] = matmul(probs, v_ref[:, span(h)])

    def level(i, number):
        return level_ref[side * half + i, number].astype(jnp.float32)

    for b in range(line_bits):

        @pl.when(bit_of(b) == 0)
        def _():
            line_state[b] = jnp.zeros(line_state.shape[1:], jnp.float32)

    copies[3].wait()
    copies[4].wait()
    for i, s in state_parts:
        at = (i, state_span(s))
        state_copy(i, s).wait_recv()
        block[0, *at] = state[side * half + i, state_span(s)] + pair_state[*at]

        @pl.when(bit_of(0) == 0)
        def _():
            line_copy(0, i, s, True).start()

    @pl.when(high_end)
    def _():
        for h in range(chunks):
            near(h)
        pass_on(0)

    for i, s in state_parts:
        at = (i, state_span(s))
        for b in range(line_bits):

            @pl.when(bit_of(b) == 1)
            def _():
                line_copy(b, i, s).wait_recv()

            if b:

                @pl.when(jnp.logical_and(bit_of(b) == 1, jnp.logical_not(ends_block(b))))
                def _():
                    line_copy(b, i, s).start()

            if b + 1 < line_bits:
                block[b + 1, *at] = block[b, *at] + line_state[b, *at]

                @pl.when(jnp.logical_and(bit_of(b + 1) == 0, ends_block(b + 1)))
                def _():
                    line_copy(b + 1, i, s, True).start()

        far = jnp.zeros((state_rows, lanes), jnp.float32)
        for b in range(line_bits):
            far = far + (level(i, 2 + b) * bit_of(b).astype(jnp.float32)) * line_state[b, *at]
        first = level(i, 1)
        right = side.astype(jnp.float32)
        mix[side * half + i, state_span(s)] = far + (first * right) * pair_state[*at]
        give[*at] = far + (first * (1.0 - right)) * state[side * half + i, state_span(s)]
        give_copy(i, s).start()

    @pl.when(jnp.logical_not(high_end))
    def _():
        for h in range(chunks):
            near(h)
            if h == 0:
                pass_on(0)

    for e in range(1, late):
        pass_on(e)

    total = jnp.zeros((tokens, lanes), jnp.float32)
    for h in range(chunks):

        @pl.when(side != h // half)
        def _():
            for s in range(STATE_PIECES):
                give_copy(h % half, s).wait_recv()

        high, low = split(mix[h])
        query = q_ref[:, span(h)]
        value = raw[h] + scale * (matmul(query, high) + matmul(query, low))
        raw[h] = value
        if h == 0:
            pair_copy(0, 0).start()
        total = total + value * value
    ones = jnp.ones((8, lanes), jnp.bfloat16)
    high, low = split(total)
    squares[...] = matmul(ones, high, NT) + matmul(ones, low, NT)
    for r in range(1, 2 * heads):
        square_copy(r).start()
    pair_copy(0, 1).start()
    grad_copy(late).start()
    for e in range(late):
        collect(0, e)
        for i in range(1, head_bits):
            if i > 1:
                collect(i - 1, e)
            forward(i, e)
    pair_copy(1, 0).start()
    grad_copy(final).start()
    for k in range(2, chunks):
        pair_copy(k, 0).start()

    def inverse_of(whole):
        root = lax.rsqrt(whole / D + 1e-06)
        return jnp.broadcast_to(root, (8, tokens)).T[:, :1]

    whole = squares[0:1]
    for r in range(1, heads):
        square_copy(r).wait_recv()
        whole = whole + squares_in[r, 0:1]
    inverse = inverse_of(whole)
    for h in range(chunks):
        normed_ref[:, span(h)] = (raw[h] * inverse).astype(jnp.bfloat16)

    def gather(e):
        pass_on(e)
        collect(0, e)
        for i in range(1, head_bits):
            if i > 1:
                collect(i - 1, e)
            forward(i, e)

    def arrive(p):
        for e in range(len(bulk)):
            if bulk[e][0] == p:
                collect(head_bits - 1, e)
        theirs_half[slots(p)] = theirs[slots(p)].astype(jnp.bfloat16)

    for p in range(last - 1):
        arrive(p)

    def product(k, p):
        flat = (group * rows, tokens)
        value = matmul(turned[side, slots(p)].reshape(flat), normed_ref[:, span(k)])
        value = value + matmul(theirs_half[slots(p)].reshape(flat), there[k])
        part[k, slots(p)] = value.reshape(group, rows, lanes)
        start = first_slot(p)

        @pl.when(high_end)
        def _():
            @pl.loop(0, group)
            def _(i):
                @pl.when(start + i < place)
                def _():
                    for q in range(slot_parts(k)):
                        down_copy(k, start + i, q).start()

        @pl.when(low_end)
        def _():
            @pl.loop(0, group)
            def _(i):
                @pl.when(start + i > place)
                def _():
                    for q in range(slot_parts(k)):
                        up_copy(k, start + i, q).start()

    def rise(k):
        @pl.loop(0, line - 1 - place)
        def _(i):
            d = line - 1 - i
            for q in range(slot_parts(k)):
                up_copy(k, d, q).wait_recv()
                part[k, d, part_span(k, q)] = part[k, d, part_span(k, q)] + rising[k, d, part_span(k, q)]
                up_copy(k, d, q).start()

    def fall(k):
        @pl.loop(0, place)
        def _(d):
            for q in range(slot_parts(k)):
                down_copy(k, d, q).wait_recv()
                part[k, d, part_span(k, q)] = part[k, d, part_span(k, q)] + falling[k, d, part_span(k, q)]
                down_copy(k, d, q).start()

    inner = jnp.logical_and(place > 0, place < line - 1)

    def nearer(k):
        @pl.when(jnp.logical_and(inner, lower))
        def _():
            rise(k)

        @pl.when(jnp.logical_and(inner, jnp.logical_not(lower)))
        def _():
            fall(k)

    def farther(k):
        @pl.when(jnp.logical_and(inner, lower))
        def _():
            fall(k)

        @pl.when(jnp.logical_and(inner, jnp.logical_not(lower)))
        def _():
            rise(k)

    alone = group == 1
    whole = jnp.zeros((1, tokens), jnp.float32)
    for r in range(heads, 2 * heads):
        square_copy(r).wait_recv()
        whole = whole + squares_in[r, 0:1]
    their_inverse = inverse_of(whole)
    for k in range(chunks):
        for t in range(pair_parts(k)):
            pair_copy(k, t).wait_recv()
        there[k] = (came[k] * their_inverse).astype(jnp.bfloat16)
        for p in range(last):
            if k == 0 and p == last - 1:
                gather(late)
                arrive(p)
            product(k, p)
        if k == 0 and alone:
            nearer(0)
        if k == 1:
            if alone:
                farther(0)
            gather(final)
            arrive(last)
            product(0, last)
            product(1, last)
            if not alone:
                nearer(0)
                farther(0)
        if k > 1:
            product(k, last)
            nearer(k - 1)
            farther(k - 1)
    nearer(chunks - 1)
    farther(chunks - 1)

    def drain(ref, sem):
        remote(ref, ref, sem, sem, {"seq": other}).wait_send()

    drain(pair_state, state_send.at[0])
    for b in range(line_bits):

        @pl.when(jnp.logical_xor(bit_of(b) == 1, ends_block(b)))
        def _():
            drain(block.at[b], state_send.at[1 + b])

    drain(give, state_send.at[1 + line_bits])
    drain(theirs, grad_send.at[0])
    drain(squares_in.at[pl.ds(1, 2 * heads - 1), pl.ds(0, 1)], square_send.at[0])
    drain(raw, pair_send.at[0])

    for k in range(chunks):
        out_ref[:, span(k)] = part[k, place]

        @pl.when(place > 0)
        def _():
            for q in range(slot_parts(k)):
                up_copy(k, place, q).wait_recv()
            out_ref[:, span(k)] = out_ref[:, span(k)] + rising[k, place]

        @pl.when(place < line - 1)
        def _():
            for q in range(slot_parts(k)):
                down_copy(k, place, q).wait_recv()
            out_ref[:, span(k)] = out_ref[:, span(k)] + falling[k, place]

    drain(part.at[:, pl.ds(0, line - 1)], slot_send.at[0])


def body(queries, keys, values, level_weights, out_grad):
    tokens, width = queries.shape
    assert tokens == GROUP
    count = lax.axis_size("seq")
    heads = lax.axis_size("head")
    line = count // 2
    line_bits = line.bit_length() - 1
    lanes = D // HEADS
    chunks = width // lanes
    half = chunks // 2
    rows = out_grad.shape[1] // count
    slots = (chunks, line, rows, lanes)
    states = (half, lanes, lanes)
    vmem = pl.BlockSpec(memory_space=pltpu.VMEM)
    away = pl.BlockSpec(memory_space=pltpu.MemorySpace.HBM)
    f32 = jnp.float32
    dma = pltpu.SemaphoreType.DMA
    return pl.pallas_call(
        functools.partial(kernel, line, heads),
        out_shape=(
            pltpu.VMEM((tokens, width), jnp.bfloat16),
            pltpu.VMEM((rows, width), f32),
        ),
        in_specs=[away] * 5,
        out_specs=(vmem, vmem),
        scratch_shapes=[
            pltpu.VMEM(queries.shape, queries.dtype),
            pltpu.VMEM(keys.shape, keys.dtype),
            pltpu.VMEM(values.shape, values.dtype),
            pltpu.VMEM(out_grad.shape, out_grad.dtype),
            pltpu.SMEM(level_weights.shape, level_weights.dtype),
            dma((5,)),
            pltpu.VMEM((chunks, lanes, lanes), f32),
            pltpu.VMEM(states, f32),
            pltpu.VMEM((line_bits, *states), f32),
            pltpu.VMEM((line_bits, *states), f32),
            pltpu.VMEM(states, f32),
            pltpu.VMEM((chunks, lanes, lanes), f32),
            pltpu.VMEM((2, line, rows, tokens), jnp.bfloat16),
            pltpu.VMEM((line, rows, tokens // heads), f32),
            pltpu.VMEM((line, rows, tokens), f32),
            pltpu.VMEM((line, rows, tokens), jnp.bfloat16),
            pltpu.VMEM((chunks, tokens, lanes), f32),
            pltpu.VMEM((chunks, tokens, lanes), f32),
            pltpu.VMEM((chunks, tokens, lanes), jnp.bfloat16),
            pltpu.VMEM((8, tokens), f32),
            pltpu.VMEM((2 * heads, 8, tokens), f32),
            pltpu.VMEM(slots, f32),
            pltpu.VMEM(slots, f32),
            pltpu.VMEM(slots, f32),
            dma((2 + line_bits,)),
            dma((2 + line_bits, half * STATE_PIECES)),
            dma((1,)),
            dma((heads, PIECES + 1)),
            dma((1,)),
            dma((2 * heads,)),
            dma((1,)),
            dma((chunks + 1,)),
            dma((1,)),
            dma(((chunks - 1) * FIRST_SLOT_PIECES + last_parts(rows), line + 1)),
        ],
        compiler_params=pltpu.CompilerParams(
            collective_id=0, has_side_effects=True, vmem_limit_bytes=60 << 20
        ),
    )(queries, keys, values, level_weights, out_grad)


def solution(mesh):
    return jax.shard_map(
        body,
        mesh=mesh,
        in_specs=(
            P("seq", "head"),
            P("seq", "head"),
            P("seq", "head"),
            P("head", None),
            P("seq", None),
        ),
        out_specs=(P("seq", "head"), P("seq", "head")),
        check_vma=False,
    )
```
